32 devices in a mesh: gx: 4 (over y, x), gy: 8 (over z, core).
Axes of the slice: x: 2, y: 2, z: 4, core: 2. Of those that a mesh axis runs over, the one named last changes fastest.
Arguments:
- adjoint_temp: float32 [128, 256, 256], P('gx', 'gy'), may hold values from -6 to 6
- adjoint_load: float32 [128, 256, 256], P('gx', 'gy'), may hold values from -6 to 6
- conductivity: float32 [3, 128, 256, 256], P(None, 'gx', 'gy'), may hold values from 0.25 to 4
- expansion: float32 [3, 128, 256, 256], P(None, 'gx', 'gy'), may hold values from 0.5 to 2
- ref_temp: float32 [128, 256, 256], P('gx', 'gy'), may hold values from -4 to 4
- wall_rows: float32 [8192, 128], P(('gx', 'gy')), may hold values from -6 to 6
- wall_dest: int32 [8192, 1], P(('gx', 'gy')), may hold values from 0 to 31; in each aligned block of 256 rows (0 to 255, 256 to 511, ...) at most 9 rows name the same one
- wall_line: int32 [8192], P(('gx', 'gy')), may hold values from 0 to 2047
- wall_count: int32 [32], P(('gx', 'gy')), may hold values from 192 to 256, as said below
- tile_owner: int32 [32, 32], P(('gx', 'gy')), may hold values from 0 to 31, each once within a row
Outputs:
- adjoint_field: float32 [128, 256, 256], P('gx', 'gy')
- block_load: float32 [32, 3, 32, 8192], P(('gx', 'gy'))
The draws below stay inside these ranges and needn't reach their ends.
Inputs may be any that keep to these rules, and one draw needn't show every extreme that they name: Each row of tile_owner names every elasticity block once. `wall_dest`: bricks are numbered with the span index slowest. Among the 256 row slots of one device, no brick is named by more than 9 of them. `wall_count`: some device has all 256 slots live.
All inputs are finite; a program needn't handle non-finite values.
Results may differ from the reference program's by a relative error of at most 0.0003.
Values sent between devices are 32-bit elements; how exact they have to be, the bound alone decides.
No kernel may reach another device: no remote copies, remote signals or barrier semaphores. Data moves between devices by JAX's collectives and lax.ppermute only.
A program may use at most 128 MiB of HBM per device.

```python
import math
from functools import reduce
import jax
import jax.numpy as jnp
import numpy as np
from jax import lax

BX = 32
BY = 32
BZ = 256
WROW = 128
ROW_DEV = 256
CAP = 9
NX = 128
NY = 256
NZ = 256
ROWS = 8192
SEGS = 2048
TILE = 8192
N_GX = 4
N_GY = 8
DEVICES = 32


def draw_wall_count(key, part):
    first_key, second_key = jax.random.split(key)
    lowest = ROW_DEV - ROW_DEV // 4
    counts = jax.random.randint(first_key, (DEVICES,), lowest, ROW_DEV + 1)
    order = jax.random.permutation(second_key, DEVICES)
    counts = counts.at[order[0]].set(ROW_DEV).at[order[1]].set(lowest)
    return counts.astype(jnp.int32)


def set_ends(entries, stream_key, smallest, largest):
    extent = entries.shape
    index_at = [jax.random.randint(jax.random.fold_in(stream_key, axis), (), 0, extent[axis]) for axis in range(len(extent))]
    entries = entries.at[tuple(index_at)].set(smallest)
    longest = extent.index(max(extent))
    index_at[longest] = (index_at[longest] + 1) % extent[longest]
    return entries.at[tuple(index_at)].set(largest)


def level_of(rng, shape, pieces, least, largest):
    level = 1.0
    for axis_at, blocks in pieces:
        heights = jax.random.uniform(jax.random.fold_in(jax.random.fold_in(rng, 6), axis_at), (blocks,), jnp.float32, least / len(pieces), largest / len(pieces))
        level = level * jnp.repeat(jnp.exp(heights), shape[axis_at] // blocks).reshape((-1,) + (1,) * (len(shape) - 1 - axis_at))
    return level


def deal_out(stream_key, own, number, rows, number_of, top, limit, slope):
    sequence = jax.random.permutation(stream_key, number_of)
    packed, common = load_shares(number_of, rows * top, limit, slope, True), load_shares(number_of, rows * top, limit, slope, False)
    places = jnp.arange(number_of)

    def named(sizes, turn):
        used = int((sizes > 0).sum())
        fixed = max(1, used // 4)
        shifted = fixed + (places - fixed + turn * (used - fixed)) % max(1, number_of - fixed)
        return jnp.zeros((number_of,), jnp.int32).at[sequence[jnp.where(places < fixed, places, shifted)]].set(jnp.asarray(sizes, jnp.int32))

    sizes = jnp.where(number % 4 == 0, named(packed, number // 4), named(common, number - number // 4 - 1))
    mixed = jax.random.permutation(jax.random.fold_in(own, 3), number_of)
    source_of, receiver = mixed[0:number_of // 2 * 2:2], mixed[1:number_of // 2 * 2:2]
    slack = jnp.minimum(sizes[source_of] - 1, limit - sizes[receiver]) // 2
    slack = jnp.where((source_of == sequence[0]) | (receiver == sequence[0]) | (sizes[receiver] == 0), 0, jnp.maximum(slack, 0))
    shifted = jax.random.randint(jax.random.fold_in(own, 4), (number_of // 2,), 0, 1 << 20) % (slack + 1)
    sizes = sizes.at[source_of].add(-shifted).at[receiver].add(shifted)
    items = jnp.searchsorted(jnp.cumsum(sizes), jnp.arange(rows * top), side="right").astype(jnp.int32)
    listing = items.reshape(top, rows).T
    listing = listing[jax.random.permutation(jax.random.fold_in(own, 1), rows)]
    turn = jax.random.randint(jax.random.fold_in(own, 2), (rows, 1), 0, top)
    return jnp.take_along_axis(listing, (jnp.arange(top)[None, :] + turn) % top, axis=1)


def load_shares(amount, total, bound, lean, full):
    portions = [(1 << 20) // math.isqrt(grade ** lean) + 1 for grade in range(1, amount + 1)]
    largest = bound if full else min(bound, max(-(-total // amount), total * portions[0] // sum(portions)))
    least = 1 if total - largest >= amount - 1 else 0
    given, spare = [largest] + [least] * (amount - 1), total - largest - least * (amount - 1)
    while spare > 0:
        candidates = [i for i in range(1, amount) if given[i] < largest] or [i for i in range(1, amount) if given[i] < bound]
        pool, budget = sum([portions[i] for i in candidates]), spare
        for i in candidates:
            addition = min(bound - given[i], max(1, budget * portions[i] // pool), spare)
            given[i] = given[i] + addition
            spare = spare - addition
    return np.array(given)


def scatter_about(stream_key, dims, scale, limit, cuts=(), kind=jnp.bfloat16):
    drawn = scale * jax.random.normal(stream_key, dims, jnp.float32)
    if cuts:
        drawn = drawn * level_of(stream_key, dims, cuts, -0.22, 0.18)
    return jnp.clip(drawn, -limit, limit).astype(kind)


def setup_inputs(seed: int = 0) -> dict:
    streams_of = jax.random.split(jax.random.key(seed), 11)
    adjoint_temp = scatter_about(streams_of[0], (NX, NY, NZ), 1.0, 6.0, ((0, 4), (1, 8)), jnp.float32)
    adjoint_load = scatter_about(streams_of[1], (NX, NY, NZ), 1.0, 6.0, ((0, 4), (1, 8)), jnp.float32)
    conductivity = jnp.clip(jnp.exp(math.log(4.0) - 2.7725887 * jax.random.uniform(streams_of[2], (3, NX, NY, NZ), jnp.float32) ** level_of(streams_of[2], (3, NX, NY, NZ), ((1, 4), (2, 8)), -0.2, 0.2)), 0.25, 4.0)
    expansion = jnp.clip(0.5 + 1.5 * jax.random.uniform(streams_of[3], (3, NX, NY, NZ), jnp.float32) ** level_of(streams_of[3], (3, NX, NY, NZ), ((1, 4), (2, 8)), -0.2, 0.2), 0.5, 2.0)
    ref_temp = scatter_about(streams_of[4], (NX, NY, NZ), 0.5, 4.0, ((0, 4), (1, 8)), jnp.float32)
    wall_rows = scatter_about(streams_of[5], (ROWS, WROW), 1.0, 6.0, ((0, 32),), jnp.float32)
    wall_dest_keys = jax.random.split(jax.random.fold_in(streams_of[6], 1), ROWS // ROW_DEV)
    wall_dest_turns = jax.random.permutation(jax.random.fold_in(streams_of[6], 3), ROWS // ROW_DEV)
    wall_dest = jax.vmap(lambda own, number: deal_out(jax.random.fold_in(streams_of[6], 2), own, number, ROW_DEV, DEVICES, 1, CAP, 2))(wall_dest_keys, wall_dest_turns).reshape((ROWS, 1))
    wall_line = set_ends(jax.random.randint(streams_of[7], (ROWS,), 0, SEGS), jax.random.fold_in(streams_of[7], 1), 0, SEGS - 1).astype(jnp.int32)
    wall_count = draw_wall_count(jax.random.fold_in(streams_of[10], 71), 0)
    tile_owner = jax.vmap(lambda own: jax.random.permutation(own, DEVICES))(jax.random.split(streams_of[9], DEVICES)).reshape((DEVICES, DEVICES)).astype(jnp.int32)
    return {"adjoint_temp": adjoint_temp, "adjoint_load": adjoint_load, "conductivity": conductivity, "expansion": expansion, "ref_temp": ref_temp, "wall_rows": wall_rows, "wall_dest": wall_dest, "wall_line": wall_line, "wall_count": wall_count, "tile_owner": tile_owner}


OMEGA = 0.8
CLASS_WEIGHTS = (1.0, 0.25, 0.125)


def sweep(field_pad, conduct_pad, source, inside):
    padded = jnp.pad(field_pad, ((0, 0), (0, 0), (1, 1)))
    conduct = jnp.pad(conduct_pad, ((0, 0), (0, 0), (0, 0), (1, 1)))
    size_x = padded.shape[0] - 2
    size_y = padded.shape[1] - 2
    size_z = padded.shape[2] - 2
    center = padded[1:-1, 1:-1, 1:-1]
    coupled = jnp.zeros(center.shape, jnp.float32)
    diagonal = jnp.zeros(center.shape, jnp.float32)
    blends = {}
    for shift_x in (-1, 0, 1):
        for shift_y in (-1, 0, 1):
            for shift_z in (-1, 0, 1):
                shifts = (shift_x, shift_y, shift_z)
                axes_set = tuple(a for a in range(3) if shifts[a] != 0)
                if len(axes_set) == 0:
                    continue
                if axes_set not in blends:
                    blends[axes_set] = reduce(lambda left, right: left + right, [conduct[a] for a in axes_set]) / float(len(axes_set))
                blended = blends[axes_set]
                local_k = blended[1:-1, 1:-1, 1:-1]
                across = lax.slice(blended, (1 + shift_x, 1 + shift_y, 1 + shift_z), (1 + shift_x + size_x, 1 + shift_y + size_y, 1 + shift_z + size_z))
                neighbour = lax.slice(padded, (1 + shift_x, 1 + shift_y, 1 + shift_z), (1 + shift_x + size_x, 1 + shift_y + size_y, 1 + shift_z + size_z))
                coupling = (0.5 * CLASS_WEIGHTS[len(axes_set) - 1]) * (local_k + across)
                coupled = coupled + coupling * (center - neighbour)
                diagonal = diagonal + coupling
    applied = center + coupled
    return (center + OMEGA * (source - applied) / (1.0 + diagonal)) * inside


def reference(adjoint_temp, adjoint_load, conductivity, expansion, ref_temp, wall_rows, wall_dest, wall_line, wall_count, tile_owner):
    devices = N_GX * N_GY
    segments = BX * BY * BZ // WROW
    row_ids = jnp.arange(ROWS, dtype=jnp.int32)
    holder = (row_ids // ROW_DEV).astype(jnp.int32)
    live = (row_ids % ROW_DEV) < wall_count[holder]
    flat = jnp.where(live, wall_dest[:, 0] * segments + wall_line, devices * segments).astype(jnp.int32)
    extra = jnp.zeros((devices * segments, WROW), jnp.float32).at[flat].add(wall_rows, mode="drop")
    extra = extra.reshape(N_GX, N_GY, BX, BY, BZ).transpose(0, 2, 1, 3, 4).reshape(NX, NY, NZ)
    source = adjoint_load + extra
    conduct_pad = jnp.pad(conductivity, ((0, 0), (1, 1), (1, 1), (0, 0)))
    first = sweep(jnp.pad(adjoint_temp, ((1, 1), (1, 1), (0, 0))), conduct_pad, source, 1.0)
    adjoint_field = sweep(jnp.pad(first, ((1, 1), (1, 1), (0, 0))), conduct_pad, source, 1.0)
    thermal_load = expansion * (adjoint_field - ref_temp)[None]
    bricks = thermal_load.reshape(3, N_GX, BX, N_GY, BY, BZ).transpose(1, 3, 0, 2, 4, 5).reshape(devices, 3, devices, TILE)
    labels = jnp.arange(devices, dtype=jnp.int32)
    matches = (tile_owner[:, :, None] == labels[None, None, :]).astype(jnp.int32)
    inverse = jnp.sum(matches * labels[None, :, None], axis=1).astype(jnp.int32)
    picked = bricks[labels[:, None], :, inverse]
    block_load = picked.transpose(1, 2, 0, 3)
    return adjoint_field, block_load
```

```python
import jax
import jax.numpy as jnp
from jax import lax
from jax.experimental import pallas as pl
from jax.experimental.pallas import tpu as pltpu
from jax.sharding import PartitionSpec as P

OMEGA = 0.8
W1, W2, W3 = 1.0, 0.25, 0.125
C2 = W2 / 2.0
C3 = W3 / 3.0
CENTRE = 2.0 * W1 + 4.0 * W2 + 8.0 * W3 / 3.0
MIB = 1 << 20
LANES = 128
F32 = jnp.float32
BF16 = jnp.bfloat16
VMEM = pltpu.MemorySpace.VMEM
SMEM = pltpu.MemorySpace.SMEM


def whole(count, space=VMEM):
    return [pl.BlockSpec(memory_space=space) for _ in range(count)]


def call(kernel, outs, scratch=(), specs=None, limit=24, name=None):
    return pl.pallas_call(
        kernel,
        out_shape=outs,
        in_specs=specs,
        out_specs=jax.tree.map(lambda _: pl.BlockSpec(memory_space=VMEM), outs),
        scratch_shapes=list(scratch),
        compiler_params=pltpu.CompilerParams(vmem_limit_bytes=limit * MIB),
        name=name,
    )


def shape(*dims):
    return jax.ShapeDtypeStruct(dims, F32)


def parts_of(value, count):
    parts = []
    for _ in range(count):
        part = value.astype(BF16)
        parts.append(part)
        value = value - part.astype(F32)
    return parts


def dot(left, right, **kw):
    return jnp.dot(left, right, preferred_element_type=F32, **kw)


def pack_kernel(count_ref, rows_ref, dest_ref, line_ref, out_ref, *, devices, capacity, pitch):
    rows_dev = rows_ref.shape[0]
    dest = dest_ref[...]
    line = line_ref[...]
    live = lax.broadcasted_iota(jnp.int32, (1, rows_dev), 1) < count_ref[0]
    brick = lax.broadcasted_iota(jnp.int32, (devices, rows_dev), 0)
    named = jnp.where((brick == dest) & live, 1.0, 0.0)
    before = lax.broadcasted_iota(jnp.int32, (rows_dev, rows_dev), 0)
    after = lax.broadcasted_iota(jnp.int32, (rows_dev, rows_dev), 1)
    earlier = dot(named.astype(BF16), jnp.where(before < after, 1.0, 0.0).astype(BF16))
    slot = jnp.sum(named * earlier, axis=0, keepdims=True).astype(jnp.int32)
    target = jnp.where(live, dest * pitch + slot, -1)
    place = lax.broadcasted_iota(jnp.int32, (devices * pitch, rows_dev), 0)
    chosen = jnp.where(place == target, 1.0, 0.0).astype(BF16)
    width = rows_ref.shape[1]
    placed = dot(chosen, jnp.concatenate(parts_of(rows_ref[...], 3), axis=1))
    out_ref[...] = placed[:, :width] + (placed[:, width : 2 * width] + placed[:, 2 * width :])
    column = lax.broadcasted_iota(jnp.int32, (width, rows_dev), 0)
    here = jnp.where((column == slot) & live, (line + 1).astype(F32), 0.0)
    lines = lax.dot_general(
        named,
        here,
        (((1,), (1,)), ((), ())),
        precision=lax.Precision.HIGHEST,
        preferred_element_type=F32,
    )
    out_ref[pl.ds(capacity, devices, stride=pitch), :] = lines


def along_z(value):
    lanes = value.shape[1]
    lane = lax.broadcasted_iota(jnp.int32, value.shape, 1)
    low = jnp.where(lane == 0, 0.0, pltpu.roll(value, 1, 1))
    high = jnp.where(lane == lanes - 1, 0.0, pltpu.roll(value, lanes - 1, 1))
    return low + high


def along_y(value):
    rows = value.shape[0]
    return pltpu.roll(value, 1, 0)[: rows - 8] + pltpu.roll(value, rows - 1, 0)[: rows - 8]


def set_rim(rim_ref, f, low, high, pad_x):
    for piece in range(rim_ref.shape[1]):
        lanes = slice(piece * LANES, (piece + 1) * LANES)
        rim_ref[f, piece, pl.ds(0, pad_x, stride=8), :] = high[:, lanes]
        rim_ref[f, piece, pl.ds(7, pad_x, stride=8), :] = low[:, lanes]


def with_rim(rim_ref, f, value, x):
    rim = [rim_ref[f, piece, pl.ds(x * 8, 8), :] for piece in range(rim_ref.shape[1])]
    return jnp.concatenate([value, jnp.concatenate(rim, axis=1)], axis=0)


def product_terms(a, b, c):
    size_y = a.shape[0] - 8
    ya, yb, yc = along_y(a), along_y(b), along_y(c)
    a, c = a[:size_y], c[:size_y]
    flat = yb + along_z(c + C2 * (yb + yc))
    side = a + C2 * (ya + yb) + along_z(C2 * (a + c) + C3 * (ya + yb + yc))
    return flat, side


def field_terms(v):
    size_y = v.shape[0] - 8
    u = along_z(v)
    yv, yu = along_y(v), along_y(u)
    v, u = v[:size_y], u[:size_y]
    ex = v + C2 * (u + yv) + C3 * yu
    ey = C2 * yv + C3 * yu
    ez = C2 * u + C3 * yu
    gy = yv + C2 * yu
    gz = u + C2 * yu
    return ex, ey, ez, gy, gz


def sweep_one_kernel(
    temp_ref, cond_ref, load_ref, xlo_ref, xhi_ref, ylo_ref, yhi_ref,
    base_ref, rate_ref, source_ref, rim_ref,
    ex_ref, ey_ref, ez_ref, sv_ref, sk_ref, pv_ref, pk_ref,
    *, size_x, size_y, pad_x,
):
    for f in range(4):
        set_rim(rim_ref, f, ylo_ref[f], yhi_ref[f], pad_x)

    def terms(values, x):
        tiles = [with_rim(rim_ref, f, values[f], x) for f in range(4)]
        v, kx, ky, kz = tiles
        ex, ey, ez, gy, gz = field_terms(v)
        flat_v, side_v = product_terms(kx * v, ky * v, kz * v)
        flat_k, side_k = product_terms(kx, ky, kz)
        ex_ref[x], ey_ref[x], ez_ref[x] = ex, ey, ez
        sv_ref[x], sk_ref[x] = side_v, side_k
        return ky[:size_y] * gy + kz[:size_y] * gz + flat_v, flat_k

    terms([xlo_ref[f] for f in range(4)], 0)
    terms([xhi_ref[f] for f in range(4)], size_x + 1)

    def first_pass(x, carry):
        at = pl.ds(pl.multiple_of(x * size_y, size_y), size_y)
        values = [temp_ref[at, :]] + [cond_ref[f, at, :] for f in range(3)]
        pv_ref[x], pk_ref[x] = terms(values, x + 1)
        return carry

    lax.fori_loop(0, size_x, first_pass, 0)

    def second_pass(x, carry):
        at = pl.ds(pl.multiple_of(x * size_y, size_y), size_y)
        kx, ky, kz = [cond_ref[f, at, :] for f in range(3)]
        h = (
            pv_ref[x]
            + kx * (ex_ref[x] + ex_ref[x + 2])
            + ky * (ey_ref[x] + ey_ref[x + 2])
            + kz * (ez_ref[x] + ez_ref[x + 2])
            + (sv_ref[x] + sv_ref[x + 2])
        )
        d = 1.0 + 0.5 * (CENTRE * (kx + ky + kz) + pk_ref[x] + (sk_ref[x] + sk_ref[x + 2]))
        rate = OMEGA / d
        load = rate * load_ref[at, :]
        rate_ref[at, :] = rate
        source_ref[at, :] = load
        base_ref[at, :] = (1.0 - OMEGA) * temp_ref[at, :] + load + (0.5 * rate) * h
        return carry

    lax.fori_loop(0, size_x, second_pass, 0)


def wall_kernel(
    got_ref, base_ref, rate_ref, source_ref,
    first_ref, total_ref, xrim_ref, yrim_ref, split_ref,
    *, devices, capacity, pitch, size_x, size_y, step,
):
    slots = devices * pitch
    width = got_ref.shape[1]
    lines = got_ref[pl.ds(capacity, devices, stride=pitch), :]
    slot = lax.broadcasted_iota(jnp.int32, (width, slots), 0)
    entry = lax.broadcasted_iota(jnp.int32, (width, slots), 1) % pitch
    spread = dot(
        lines,
        jnp.where((slot == entry) & (slot < capacity), 1.0, 0.0),
        precision=lax.Precision.HIGHEST,
    )
    holder = lax.broadcasted_iota(jnp.int32, (devices, slots), 0)
    own = lax.broadcasted_iota(jnp.int32, (devices, slots), 1) // pitch
    line = jnp.sum(jnp.where(holder == own, spread, 0.0), axis=0, keepdims=True).astype(jnp.int32) - 1
    parts = jnp.concatenate(parts_of(got_ref[...], 3), axis=1)
    lanes = base_ref.shape[1]
    pieces = lanes // width

    def block(i, carry):
        at = pl.ds(pl.multiple_of(i * step, step), step)
        cell = lax.broadcasted_iota(jnp.int32, (step, slots), 0) + i * step
        walls = []
        for piece in range(pieces):
            chosen = jnp.where(cell * pieces + piece == line, 1.0, 0.0).astype(BF16)
            wall = dot(chosen, parts)
            walls.append(wall[:, :width] + (wall[:, width : 2 * width] + wall[:, 2 * width :]))
        added = rate_ref[at, :] * jnp.concatenate(walls, axis=1)
        first = base_ref[at, :] + added
        first_ref[at, :] = first
        for piece in range(pieces):
            split_ref[piece, at, :] = first[:, piece * width : (piece + 1) * width]
        total_ref[at, :] = source_ref[at, :] + added
        return carry

    lax.fori_loop(0, base_ref.shape[0] // step, block, 0)
    xrim_ref[0] = first_ref[pl.ds(0, size_y), :]
    xrim_ref[1] = first_ref[pl.ds((size_x - 1) * size_y, size_y), :]
    for piece in range(pieces):
        at = slice(piece * width, (piece + 1) * width)
        yrim_ref[0, :, at] = split_ref[piece, pl.ds(0, size_x, stride=size_y), :]
        yrim_ref[1, :, at] = split_ref[piece, pl.ds(size_y - 1, size_x, stride=size_y), :]


def sweep_two_kernel(
    owner_ref, first_ref, cond_ref, rate_ref, total_ref, reft_ref, expand_ref,
    xlo_ref, xhi_ref, ylo_ref, yhi_ref, fxlo_ref, fxhi_ref, fylo_ref, fyhi_ref,
    field_ref, late_ref,
    rim_ref, ex_ref, ey_ref, ez_ref, sv_ref, pv_ref,
    *, size_x, size_y, pad_x, tile_rows,
):
    set_rim(rim_ref, 0, fylo_ref[0], fyhi_ref[0], pad_x)
    for f in range(1, 4):
        set_rim(rim_ref, f, ylo_ref[f], yhi_ref[f], pad_x)

    def terms(values, x):
        tiles = [with_rim(rim_ref, f, values[f], x) for f in range(4)]
        v, kx, ky, kz = tiles
        ex, ey, ez, gy, gz = field_terms(v)
        flat_v, side_v = product_terms(kx * v, ky * v, kz * v)
        ex_ref[x], ey_ref[x], ez_ref[x] = ex, ey, ez
        sv_ref[x] = side_v
        return ky[:size_y] * gy + kz[:size_y] * gz + flat_v

    terms([fxlo_ref[0]] + [xlo_ref[f] for f in range(1, 4)], 0)
    terms([fxhi_ref[0]] + [xhi_ref[f] for f in range(1, 4)], size_x + 1)

    def first_pass(x, carry):
        at = pl.ds(pl.multiple_of(x * size_y, size_y), size_y)
        values = [first_ref[at, :]] + [cond_ref[f, at, :] for f in range(3)]
        pv_ref[x] = terms(values, x + 1)
        return carry

    lax.fori_loop(0, size_x, first_pass, 0)
    per_plane = size_y // tile_rows

    def second_pass(x, carry):
        at = pl.ds(pl.multiple_of(x * size_y, size_y), size_y)
        kx, ky, kz = [cond_ref[f, at, :] for f in range(3)]
        h = (
            pv_ref[x]
            + kx * (ex_ref[x] + ex_ref[x + 2])
            + ky * (ey_ref[x] + ey_ref[x + 2])
            + kz * (ez_ref[x] + ez_ref[x + 2])
            + (sv_ref[x] + sv_ref[x + 2])
        )
        field = (1.0 - OMEGA) * first_ref[at, :] + total_ref[at, :] + (0.5 * rate_ref[at, :]) * h
        field_ref[at, :] = field
        strain = field - reft_ref[at, :]
        for part in range(per_plane):
            owner = owner_ref[0, x * per_plane + part]
            rows = slice(part * tile_rows, (part + 1) * tile_rows)
            for c in range(3):
                load = (expand_ref[c, at, :] * strain)[rows]
                for piece in range(late_ref.shape[2]):
                    late_ref[owner, c, piece] = load[:, piece * LANES : (piece + 1) * LANES]
        return carry

    lax.fori_loop(0, size_x, second_pass, 0)


def settle_kernel(late_ref, out_ref, *, tile_rows, pieces):
    c, block = pl.program_id(0), pl.program_id(1)
    pitch = 3 * pieces * tile_rows
    for y in range(tile_rows):
        for piece in range(pieces):
            start = block * 8 * pitch + (c * pieces + piece) * tile_rows + y
            lane = (y * pieces + piece) * LANES
            out_ref[0, 0, :, lane : lane + LANES] = late_ref[pl.ds(start, 8, stride=pitch), :]


def neighbours(axis):
    count = lax.axis_size(axis)
    up = [(i, i + 1) for i in range(count - 1)]
    return up, [(b, a) for a, b in up]


def body(
    adjoint_temp, adjoint_load, conductivity, expansion, ref_temp,
    wall_rows, wall_dest, wall_line, wall_count, tile_owner,
):
    axes = ("gx", "gy")
    devices = lax.axis_size("gx") * lax.axis_size("gy")
    size_x, size_y, size_z = adjoint_temp.shape
    rows_dev, width = wall_rows.shape
    cells = size_x * size_y
    capacity = (rows_dev + devices - 1) // devices + 1
    pitch = (capacity + 1 + 7) // 8 * 8
    pad_x = size_x + 8
    tile_rows = cells // devices
    up_x, down_x = neighbours("gx")
    up_y, down_y = neighbours("gy")

    packed = call(
        lambda *refs: pack_kernel(*refs, devices=devices, capacity=capacity, pitch=pitch),
        shape(devices * pitch, width),
        specs=whole(1, SMEM) + whole(3),
        name="pack_rows",
    )(wall_count, wall_rows, wall_dest.reshape(1, rows_dev), wall_line.reshape(1, rows_dev))
    got = lax.all_to_all(
        packed.reshape(devices, pitch, width), axes, split_axis=0, concat_axis=0, tiled=True
    ).reshape(devices * pitch, width)

    stacked = lambda at: jnp.concatenate([adjoint_temp[at][None], conductivity[:, at]], axis=0)
    xlo = lax.ppermute(stacked(size_x - 1), "gx", up_x)
    xhi = lax.ppermute(stacked(0), "gx", down_x)

    def edge(at):
        lines = jnp.concatenate([adjoint_temp[None, :, at], conductivity[:, :, at]], axis=0)
        return jnp.concatenate(
            [xlo[:, None, at], lines, xhi[:, None, at], jnp.zeros((4, pad_x - size_x - 2, size_z), F32)],
            axis=1,
        )

    ylo = lax.ppermute(edge(size_y - 1), "gy", up_y)
    yhi = lax.ppermute(edge(0), "gy", down_y)

    flat = lambda array: array.reshape(array.shape[:-3] + (cells, size_z))
    temp, cond, load = flat(adjoint_temp), flat(conductivity), flat(adjoint_load)
    plane = pltpu.VMEM((size_x, size_y, size_z), F32)
    wide = pltpu.VMEM((size_x + 2, size_y, size_z), F32)
    pieces = size_z // LANES
    rims = pltpu.VMEM((4, pieces, pad_x * 8, LANES), F32)
    grid = shape(cells, size_z)
    base, rate, source = call(
        lambda *refs: sweep_one_kernel(*refs, size_x=size_x, size_y=size_y, pad_x=pad_x),
        (grid, grid, grid),
        scratch=[rims] + [wide] * 5 + [plane] * 2,
        specs=whole(7),
        limit=40,
        name="sweep_one",
    )(temp, cond, load, xlo, xhi, ylo, yhi)
    first, total, xrim, yrim = call(
        lambda *refs: wall_kernel(
            *refs, devices=devices, capacity=capacity, pitch=pitch,
            size_x=size_x, size_y=size_y, step=cells // 8,
        ),
        (grid, grid, shape(2, size_y, size_z), shape(2, size_x, size_z)),
        scratch=[pltpu.VMEM((pieces, cells, LANES), F32)],
        specs=whole(4),
        name="wall_source",
    )(got, base, rate, source)

    fxlo = lax.ppermute(xrim[1:2], "gx", up_x)
    fxhi = lax.ppermute(xrim[0:1], "gx", down_x)

    def rim_edge(side, at):
        return jnp.concatenate(
            [fxlo[:, at : at + 1], yrim[side : side + 1], fxhi[:, at : at + 1],
             jnp.zeros((1, pad_x - size_x - 2, size_z), F32)],
            axis=1,
        )

    fylo = lax.ppermute(rim_edge(1, size_y - 1), "gy", up_y)
    fyhi = lax.ppermute(rim_edge(0, 0), "gy", down_y)

    field, late = call(
        lambda *refs: sweep_two_kernel(
            *refs, size_x=size_x, size_y=size_y, pad_x=pad_x, tile_rows=tile_rows
        ),
        (grid, shape(devices, 3, pieces, tile_rows, LANES)),
        scratch=[rims] + [wide] * 4 + [plane],
        specs=whole(1, SMEM) + whole(14),
        limit=40,
        name="sweep_two",
    )(tile_owner, first, cond, rate, total, flat(ref_temp), flat(expansion),
      xlo, xhi, ylo, yhi, fxlo, fxhi, fylo, fyhi)

    moved = lax.all_to_all(late, axes, split_axis=0, concat_axis=0, tiled=True)
    tile_cells = tile_rows * size_z
    block_load = pl.pallas_call(
        lambda *refs: settle_kernel(*refs, tile_rows=tile_rows, pieces=pieces),
        out_shape=shape(1, 3, devices, tile_cells),
        grid=(3, devices // 8),
        in_specs=whole(1),
        out_specs=pl.BlockSpec((1, 1, 8, tile_cells), lambda c, b: (0, c, b, 0)),
        compiler_params=pltpu.CompilerParams(vmem_limit_bytes=16 * MIB),
        name="settle",
    )(moved.reshape(devices * 3 * pieces * tile_rows, LANES))
    return field.reshape(size_x, size_y, size_z), block_load


def solution(mesh):
    placed = (
        P("gx", "gy", None),
        P("gx", "gy", None),
        P(None, "gx", "gy", None),
        P(None, "gx", "gy", None),
        P("gx", "gy", None),
        P(("gx", "gy"), None),
        P(("gx", "gy"), None),
        P(("gx", "gy")),
        P(("gx", "gy")),
        P(("gx", "gy"), None),
    )
    return jax.shard_map(
        body,
        mesh=mesh,
        in_specs=placed,
        out_specs=(P("gx", "gy", None), P(("gx", "gy"), None, None, None)),
        check_vma=False,
    )
```

```python
import jax
import jax.numpy as jnp
from jax import lax
from jax.experimental import pallas as pl
from jax.experimental.pallas import tpu as pltpu
from jax.sharding import PartitionSpec as P


OMEGA = 0.8
W1, W2, W3 = 1.0, 0.25, 0.125
C2 = W2 / 2.0
C3 = W3 / 3.0
CENTRE = 2.0 * W1 + 4.0 * W2 + 8.0 * W3 / 3.0
MIB = 1 << 20
LANES = 128
CORNER_ROWS = 3
EARLY_EIGHTHS = 2
GROUPS = 4
AXES = ("gx", "gy")
F32 = jnp.float32
BF16 = jnp.bfloat16
VMEM = pltpu.MemorySpace.VMEM
SMEM = pltpu.MemorySpace.SMEM
HBM = pltpu.MemorySpace.HBM


def whole(count, space=VMEM):
    return [pl.BlockSpec(memory_space=space) for _ in range(count)]


def call(kernel, outs, scratch=(), specs=None, limit=60):
    return pl.pallas_call(
        kernel,
        out_shape=outs,
        in_specs=specs,
        out_specs=jax.tree.map(lambda _: pl.BlockSpec(memory_space=HBM), outs),
        scratch_shapes=list(scratch),
        compiler_params=pltpu.CompilerParams(vmem_limit_bytes=limit * MIB),
    )


def shape(*dims):
    return jax.ShapeDtypeStruct(dims, F32)


def parts_of(value, count):
    parts = []
    for _ in range(count):
        part = value.astype(BF16)
        parts.append(part)
        value = value - part.astype(F32)
    return parts


def dot(left, right, **kw):
    return jnp.dot(left, right, preferred_element_type=F32, **kw)


def lanes_of(piece):
    return slice(piece * LANES, (piece + 1) * LANES)


def split(value):
    return [value[:, lanes_of(p)] for p in range(value.shape[1] // LANES)]


def diagonal(move_x, move_y):
    count_x, count_y = lax.axis_size("gx"), lax.axis_size("gy")
    at_x, at_y = lax.axis_index("gx") + move_x, lax.axis_index("gy") + move_y
    there = (at_x >= 0) & (at_x < count_x) & (at_y >= 0) & (at_y < count_y)
    return jnp.where(there, at_x * count_y + at_y, 0), there


CORNERS = [(-1, -1), (-1, 1), (1, -1), (1, 1)]


def fetch(pairs, sems, start=0):
    copies = [pltpu.make_async_copy(src, dst, sems.at[start + i]) for i, (src, dst) in enumerate(pairs)]
    for copy in copies:
        copy.start()
    return copies


def wait(copies):
    for copy in copies:
        copy.wait()


def prepare_kernel(
    count_ref, rows_hbm, dest_hbm, line_hbm, temp_hbm, cond_hbm,
    packed_hbm, below_hbm, above_hbm, low_hbm, high_hbm,
    rows_ref, dest_ref, line_ref, outer_ref, sides_ref, out_ref, low_ref, high_ref, sems,
    *, devices, capacity, pitch, size_x, size_y,
):
    fields = [temp_hbm] + [cond_hbm.at[f] for f in range(3)]
    small = fetch([(rows_hbm, rows_ref), (dest_hbm, dest_ref), (line_hbm, line_ref)], sems)
    wanted = []
    for f, field in enumerate(fields):
        for side, x in enumerate((0, size_x - 1)):
            wanted.append((field.at[x], outer_ref.at[side, f]))
        for side, y in enumerate((0, size_y - 8)):
            wanted.append((field.at[:, pl.ds(y, 8), :], sides_ref.at[side, f]))
    large = fetch(wanted, sems, 3)
    wait(small)

    rows_dev, width = rows_ref.shape
    dest = dest_ref[...]
    line = line_ref[...]
    live = lax.broadcasted_iota(jnp.int32, (1, rows_dev), 1) < count_ref[0]
    brick = lax.broadcasted_iota(jnp.int32, (devices, rows_dev), 0)
    named = jnp.where((brick == dest) & live, 1.0, 0.0)
    before = lax.broadcasted_iota(jnp.int32, (rows_dev, rows_dev), 0)
    after = lax.broadcasted_iota(jnp.int32, (rows_dev, rows_dev), 1)
    earlier = dot(named.astype(BF16), jnp.where(before < after, 1.0, 0.0).astype(BF16))
    slot = jnp.sum(named * earlier, axis=0, keepdims=True).astype(jnp.int32)
    target = jnp.where(live, dest * pitch + slot, -1)
    place = lax.broadcasted_iota(jnp.int32, (devices * pitch, rows_dev), 0)
    chosen = jnp.where(place == target, 1.0, 0.0).astype(BF16)
    placed = dot(chosen, jnp.concatenate(parts_of(rows_ref[...], 3), axis=1))
    out_ref[...] = placed[:, :width] + (placed[:, width : 2 * width] + placed[:, 2 * width :])
    column = lax.broadcasted_iota(jnp.int32, (width, rows_dev), 0)
    here = jnp.where((column == slot) & live, (line + 1).astype(F32), 0.0)
    lines = lax.dot_general(
        named,
        here,
        (((1,), (1,)), ((), ())),
        precision=lax.Precision.HIGHEST,
        preferred_element_type=F32,
    )
    out_ref[pl.ds(capacity, devices, stride=pitch), :] = lines

    wait(large)
    for move_x, move_y in CORNERS:
        brick, there = diagonal(move_x, move_y)
        side, row = (0 if move_x < 0 else 1), (0 if move_y < 0 else size_y - 1)
        v, kx, ky, kz = [outer_ref[side, f, row : row + 1, :] for f in range(4)]

        @pl.when(there)
        def _():
            row = brick * pitch + capacity + 1
            for value in (v, kx + ky, kz):
                for part in split(value):
                    out_ref[pl.ds(row, 1), :] = part
                    row = row + 1

    sent = fetch([(out_ref, packed_hbm), (outer_ref.at[0], below_hbm), (outer_ref.at[1], above_hbm)], sems)
    for f in range(4):
        for x in range(size_x):
            low_ref[f, x : x + 1, :] = sides_ref[0, f, x, 0:1, :]
            high_ref[f, x : x + 1, :] = sides_ref[1, f, x, 7:8, :]
    wait(sent + fetch([(low_ref, low_hbm), (high_ref, high_hbm)], sems, 3))


def along_z(pieces):
    lane = lax.broadcasted_iota(jnp.int32, pieces[0].shape, 1)
    up = [pltpu.roll(p, 1, 1) for p in pieces]
    down = [pltpu.roll(p, LANES - 1, 1) for p in pieces]
    last = len(pieces) - 1
    return [
        jnp.where(lane == 0, up[i - 1] if i > 0 else 0.0, up[i])
        + jnp.where(lane == LANES - 1, down[i + 1] if i < last else 0.0, down[i])
        for i in range(last + 1)
    ]


def along_y(pieces):
    rows = pieces[0].shape[0]
    return [pltpu.roll(p, 1, 0)[: rows - 8] + pltpu.roll(p, rows - 1, 0)[: rows - 8] for p in pieces]


def each(function, *lists):
    return [function(*values) for values in zip(*lists)]


def inner(pieces):
    return [p[: p.shape[0] - 8] for p in pieces]


def product_terms(a, b, c, side_only=False):
    ya, yb, yc = along_y(a), along_y(b), along_y(c)
    a, c = inner(a), inner(c)
    yab = each(lambda s, t: s + t, ya, yb)
    side_z = along_z(each(lambda a, c, yab, yc: C2 * (a + c) + C3 * (yab + yc), a, c, yab, yc))
    side = each(lambda a, yab, z: a + C2 * yab + z, a, yab, side_z)
    if side_only:
        return None, side
    flat_z = along_z(each(lambda c, yb, yc: c + C2 * (yb + yc), c, yb, yc))
    return each(lambda yb, z: yb + z, yb, flat_z), side


def field_terms(v):
    u = along_z(v)
    yv, yu = along_y(v), along_y(u)
    v, u = inner(v), inner(u)
    c3yu = each(lambda yu: C3 * yu, yu)
    ey = each(lambda yv, t: C2 * yv + t, yv, c3yu)
    c2u = each(lambda u: C2 * u, u)
    ez = each(lambda s, t: s + t, c2u, c3yu)
    ex = each(lambda v, s, t: v + s + t, v, c2u, ey)
    c2yu = each(lambda yu: C2 * yu, yu)
    gy = each(lambda yv, t: yv + t, yv, c2yu)
    gz = each(lambda u, t: u + t, u, c2yu)
    return ex, ey, ez, gy, gz


def put(ref, x, pieces):
    for p, value in enumerate(pieces):
        ref[x, :, lanes_of(p)] = value


def set_rim(rim_ref, f, low, high, size_x):
    for p in range(rim_ref.shape[1]):
        rim_ref[f, p, pl.ds(8, size_x, stride=8), :] = high[:, lanes_of(p)]
        rim_ref[f, p, pl.ds(15, size_x, stride=8), :] = low[:, lanes_of(p)]


def with_rim(rim_ref, f, value, x):
    return [
        jnp.concatenate([piece, rim_ref[f, p, pl.ds(x * 8, 8), :]], axis=0)
        for p, piece in enumerate(split(value))
    ]


def plane_terms(tiles, x, terms_refs, side_only=False):
    v, kx, ky, kz = tiles
    ex, ey, ez, gy, gz = field_terms(v)
    times = lambda k: each(lambda k, v: k * v, k, v)
    flat, side = product_terms(times(kx), times(ky), times(kz), side_only)
    for ref, value in zip(terms_refs, (ex, ey, ez, side)):
        put(ref, x, value)
    if side_only:
        return None
    return each(lambda ky, gy, kz, gz, f: ky * gy + kz * gz + f, inner(ky), gy, inner(kz), gz, flat)


def coupled(k, partial, before, after):
    both = [low[...] + high[...] for low, high in zip(before, after)]
    return partial + k[0] * both[0] + k[1] * both[1] + k[2] * both[2] + both[3]


def first_kernel(
    temp_hbm, cond_hbm, load_hbm, xlo_hbm, xhi_hbm, ylo_hbm, yhi_hbm, got_hbm,
    first_hbm, total_hbm, rate_hbm, krim_hbm, low_hbm, high_hbm,
    temp_ref, cond_ref, load_ref, first_ref, total_ref, rate_ref, rim_ref, low_ref, high_ref,
    ex_ref, ey_ref, ez_ref, sv_ref, sk_ref, pv_ref, pk_ref,
    outer_ref, ylo_ref, yhi_ref, got_ref, parts_ref, split_ref, sems,
    *, devices, size_x, size_y, capacity, pitch, step, groups,
):
    copies = fetch(
        [(ylo_hbm, ylo_ref), (yhi_hbm, yhi_ref), (got_hbm, got_ref),
         (xlo_hbm, outer_ref.at[0]), (xhi_hbm, outer_ref.at[1])], sems,
    )
    rows = first_ref.shape[0] // groups
    part = lambda g: pl.ds(g * rows, rows)
    loads = [
        fetch([(temp_hbm.at[part(g)], temp_ref.at[part(g)]), (cond_hbm.at[:, part(g)], cond_ref.at[:, part(g)])],
              sems, 5 + 2 * g)
        for g in range(groups)
    ]
    load = fetch([(load_hbm, load_ref)], sems, 5 + 2 * groups)
    wait(copies)
    pieces = rim_ref.shape[1]
    for f in range(4):
        set_rim(rim_ref, f, ylo_ref[f], yhi_ref[f], size_x)
    for move_x, move_y in CORNERS:
        brick, there = diagonal(move_x, move_y)
        row = brick * pitch + capacity + 1
        at = (0 if move_x < 0 else size_x + 1) * 8 + (7 if move_y < 0 else 0)
        for p in range(pieces):
            for i, f in enumerate((0, 1, 3)):
                value = got_ref[pl.ds(row + i * pieces + p, 1), :]
                rim_ref[f, p, at : at + 1, :] = jnp.where(there, value, 0.0)
            rim_ref[2, p, at : at + 1, :] = jnp.zeros((1, LANES), F32)
    sent = fetch([(rim_ref, krim_hbm)], sems)

    def terms(values, x, side_only=False):
        tiles = [with_rim(rim_ref, f, values[f], x) for f in range(4)]
        partial = plane_terms(tiles, x, (ex_ref, ey_ref, ez_ref, sv_ref), side_only)
        flat, side = product_terms(*tiles[1:], side_only)
        put(sk_ref, x, side)
        return partial, flat

    terms([outer_ref[0, f] for f in range(4)], 0, True)
    terms([outer_ref[1, f] for f in range(4)], size_x + 1, True)

    def first_pass(x, carry):
        at = pl.ds(pl.multiple_of(x * size_y, size_y), size_y)
        values = [temp_ref[at, :]] + [cond_ref[f, at, :] for f in range(3)]
        partial, flat = terms(values, x + 1)
        put(pv_ref, x, partial)
        put(pk_ref, x, flat)
        return carry

    each_group = size_x // groups
    for g in range(groups):
        wait(loads[g])
        lax.fori_loop(g * each_group, (g + 1) * each_group, first_pass, 0)
    wait(load)

    def second_pass(x, carry):
        at = pl.ds(pl.multiple_of(x * size_y, size_y), size_y)
        k = [cond_ref[f, at, :] for f in range(3)]
        refs = (ex_ref, ey_ref, ez_ref, sv_ref)
        h = coupled(k, pv_ref[x], [r.at[x] for r in refs], [r.at[x + 2] for r in refs])
        d = 1.0 + 0.5 * (CENTRE * (k[0] + k[1] + k[2]) + pk_ref[x] + (sk_ref[x] + sk_ref[x + 2]))
        rate = OMEGA / d
        load = rate * load_ref[at, :]
        rate_ref[at, :] = rate
        total_ref[at, :] = load
        first_ref[at, :] = (1.0 - OMEGA) * temp_ref[at, :] + load + (0.5 * rate) * h
        return carry

    lax.fori_loop(0, size_x, second_pass, 0)

    slots = devices * pitch
    width = got_ref.shape[1]
    lines = got_ref[pl.ds(capacity, devices, stride=pitch), :]
    slot = lax.broadcasted_iota(jnp.int32, (width, slots), 0)
    entry = lax.broadcasted_iota(jnp.int32, (width, slots), 1) % pitch
    spread = dot(
        lines,
        jnp.where((slot == entry) & (slot < capacity), 1.0, 0.0),
        precision=lax.Precision.HIGHEST,
    )
    holder = lax.broadcasted_iota(jnp.int32, (devices, slots), 0)
    own = lax.broadcasted_iota(jnp.int32, (devices, slots), 1) // pitch
    line = jnp.sum(jnp.where(holder == own, spread, 0.0), axis=0, keepdims=True).astype(jnp.int32) - 1
    parts_ref[...] = jnp.concatenate(parts_of(got_ref[...], 2), axis=1)

    def block(i, carry):
        at = pl.ds(pl.multiple_of(i * step, step), step)
        cell = lax.broadcasted_iota(jnp.int32, (step, slots), 0) + i * step
        for piece in range(pieces):
            chosen = jnp.where(cell * pieces + piece == line, 1.0, 0.0).astype(BF16)
            wall = dot(chosen, parts_ref[...])
            lanes = lanes_of(piece)
            added = rate_ref[at, lanes] * (wall[:, :width] + wall[:, width:])
            first = first_ref[at, lanes] + added
            first_ref[at, lanes] = first
            split_ref[piece, at, :] = first
            total_ref[at, lanes] = total_ref[at, lanes] + added
        return carry

    steps = first_ref.shape[0] // step // groups
    for g in range(groups):
        lax.fori_loop(g * steps, (g + 1) * steps, block, 0)
        sent += fetch(
            [(ref.at[part(g)], hbm.at[part(g)])
             for ref, hbm in ((first_ref, first_hbm), (total_ref, total_hbm), (rate_ref, rate_hbm))],
            sems, 1 + 3 * g,
        )
    for piece in range(pieces):
        low_ref[:, lanes_of(piece)] = split_ref[piece, pl.ds(0, size_x, stride=size_y), :]
        high_ref[:, lanes_of(piece)] = split_ref[piece, pl.ds(size_y - 1, size_x, stride=size_y), :]
    wait(sent + fetch([(low_ref, low_hbm), (high_ref, high_hbm)], sems, 1 + 3 * groups))


def planes_kernel(first_hbm, ylo_hbm, yhi_hbm, below_hbm, above_hbm, ylo_ref, yhi_ref, send_ref, sems, *, size_x, size_y):
    copies = fetch([(ylo_hbm, ylo_ref), (yhi_hbm, yhi_ref)], sems)
    for side, x in enumerate((0, size_x - 1)):
        copies += fetch(
            [(first_hbm.at[pl.ds(x * size_y, size_y)], send_ref.at[side, pl.ds(0, size_y)])], sems, 2 + side
        )
    wait(copies)
    for side, x in enumerate((0, size_x - 1)):
        send_ref[side, size_y : size_y + 1] = yhi_ref[x : x + 1, :]
        send_ref[side, size_y + 7 : size_y + 8] = ylo_ref[x : x + 1, :]
    wait(fetch([(send_ref.at[0], below_hbm), (send_ref.at[1], above_hbm)], sems))


def field_kernel(
    owner_ref, first_hbm, cond_hbm, rate_hbm, total_hbm, reft_hbm, expand_hbm,
    xlo_hbm, xhi_hbm, krim_hbm, ylo_hbm, yhi_hbm, fxlo_hbm, fxhi_hbm,
    field_hbm, late_hbm,
    first_ref, cond_ref, rate_ref, total_ref, reft_ref, expand_ref, field_ref, stage_ref,
    outer_ref, rim_ref, ylo_ref, yhi_ref, planes_ref,
    ex_ref, ey_ref, ez_ref, sv_ref, pv_ref, sems, late_sem,
    *, size_x, size_y, tile_rows, early_rows, groups,
):
    copies = fetch(
        [(ylo_hbm, ylo_ref), (yhi_hbm, yhi_ref), (krim_hbm, rim_ref),
         (xlo_hbm, outer_ref.at[0]), (xhi_hbm, outer_ref.at[1]),
         (fxlo_hbm, planes_ref.at[0]), (fxhi_hbm, planes_ref.at[1])], sems,
    )
    rows = first_ref.shape[0] // groups
    part = lambda g: pl.ds(g * rows, rows)
    loads = [
        fetch([(first_hbm.at[part(g)], first_ref.at[part(g)]), (cond_hbm.at[:, part(g)], cond_ref.at[:, part(g)])],
              sems, 7 + 2 * g)
        for g in range(groups)
    ]
    later = fetch(
        [(rate_hbm, rate_ref), (total_hbm, total_ref), (reft_hbm, reft_ref), (expand_hbm, expand_ref)],
        sems, 7 + 2 * groups,
    )
    wait(copies)
    set_rim(rim_ref, 0, ylo_ref, yhi_ref, size_x)
    refs = (ex_ref, ey_ref, ez_ref, sv_ref)
    for side, x in enumerate((0, size_x + 1)):
        tiles = [split(planes_ref[side])]
        tiles += [with_rim(rim_ref, f, outer_ref[side, f], x) for f in range(1, 4)]
        plane_terms(tiles, x, refs, True)

    def first_pass(x, carry):
        at = pl.ds(pl.multiple_of(x * size_y, size_y), size_y)
        values = [first_ref[at, :]] + [cond_ref[f, at, :] for f in range(3)]
        tiles = [with_rim(rim_ref, f, values[f], x + 1) for f in range(4)]
        put(pv_ref, x, plane_terms(tiles, x + 1, refs))
        return carry

    each_group = size_x // groups
    for g in range(groups):
        wait(loads[g])
        lax.fori_loop(g * each_group, (g + 1) * each_group, first_pass, 0)
    wait(later)
    per_plane = size_y // tile_rows
    kept = tile_rows - early_rows

    def second_pass(x, carry):
        at = pl.ds(pl.multiple_of(x * size_y, size_y), size_y)
        k = [cond_ref[f, at, :] for f in range(3)]
        h = coupled(k, pv_ref[x], [r.at[x] for r in refs], [r.at[x + 2] for r in refs])
        field = (1.0 - OMEGA) * first_ref[at, :] + total_ref[at, :] + (0.5 * rate_ref[at, :]) * h
        field_ref[at, :] = field
        strain = field - reft_ref[at, :]
        for p in range(per_plane):
            tile = x * per_plane + p
            start = p * tile_rows
            early, end = start + early_rows, start + tile_rows
            if early_rows:
                stage_ref[tile, :early_rows] = strain[start:early]
            for c in range(3 if kept else 0):
                low = early_rows + c * kept
                stage_ref[tile, low : low + kept] = (expand_ref[c, at, :] * strain)[early:end]
            pltpu.make_async_copy(stage_ref.at[tile], late_hbm.at[owner_ref[0, tile]], late_sem).start()
        return carry

    sent = []
    for g in range(groups):
        lax.fori_loop(g * each_group, (g + 1) * each_group, second_pass, 0)
        sent += fetch([(field_ref.at[part(g)], field_hbm.at[part(g)])], sems, g)
    wait(sent)
    pltpu.make_async_copy(stage_ref, late_hbm, late_sem).wait()


def early_kernel(owner_ref, expand_hbm, out_hbm, stage_ref, in_sems, sem, *, tile_rows, early_rows, groups):
    tiles = stage_ref.shape[0] // groups
    loads = []
    for g in range(groups):
        for j in range(g * tiles, (g + 1) * tiles):
            loads.append(
                pltpu.make_async_copy(
                    expand_hbm.at[:, pl.ds(j * tile_rows, early_rows)], stage_ref.at[j], in_sems.at[g]
                )
            )
            loads[-1].start()
    for g in range(groups):
        wait(loads[g * tiles : (g + 1) * tiles])
        for j in range(g * tiles, (g + 1) * tiles):
            pltpu.make_async_copy(stage_ref.at[j], out_hbm.at[owner_ref[0, j]], sem).start()
    pltpu.make_async_copy(stage_ref, out_hbm, sem).wait()


def settle_kernel(*refs, tile_rows, early_rows, pieces):
    late, early, out_ref = refs[:pieces], refs[pieces:-1], refs[-1]
    kept = tile_rows - early_rows
    pitch = early_rows + 3 * kept
    lane = lambda y, p: slice((y * pieces + p) * LANES, (y * pieces + p + 1) * LANES)
    for p in range(pieces):
        for y in range(early_rows):
            strain = late[p][pl.ds(y, 8, stride=pitch), :]
            for c in range(3):
                factor = early[p][pl.ds(c * early_rows + y, 8, stride=3 * early_rows), :]
                out_ref[0, c, :, lane(y, p)] = factor * strain
        for c in range(3):
            for y in range(kept):
                at = early_rows + c * kept + y
                out_ref[0, c, :, lane(early_rows + y, p)] = late[p][pl.ds(at, 8, stride=pitch), :]


def neighbours(axis):
    count = lax.axis_size(axis)
    up = [(i, i + 1) for i in range(count - 1)]
    return up, [(b, a) for a, b in up]


def body(
    adjoint_temp, adjoint_load, conductivity, expansion, ref_temp,
    wall_rows, wall_dest, wall_line, wall_count, tile_owner,
):
    devices = lax.axis_size("gx") * lax.axis_size("gy")
    size_x, size_y, size_z = adjoint_temp.shape
    rows_dev, width = wall_rows.shape
    cells = size_x * size_y
    pieces = size_z // LANES
    capacity = (rows_dev + devices - 1) // devices + 1
    pitch = (capacity + 1 + CORNER_ROWS * pieces + 7) // 8 * 8
    tile_rows = cells // devices
    early_rows = tile_rows // 8 * EARLY_EIGHTHS // 8 * 8
    kept = tile_rows - early_rows
    up_x, down_x = neighbours("gx")
    up_y, down_y = neighbours("gy")
    exchange = lambda array: lax.all_to_all(array, AXES, split_axis=0, concat_axis=0, tiled=True)
    flat = lambda array: array.reshape(array.shape[:-3] + (cells, size_z))
    temp, cond, load, expand = map(flat, (adjoint_temp, conductivity, adjoint_load, expansion))

    buffer = lambda *dims: pltpu.VMEM(dims, F32)
    sems = lambda count: pltpu.SemaphoreType.DMA((count,))
    grid, lines = shape(cells, size_z), shape(size_x, size_z)

    packed, below, above, low, high = call(
        lambda *refs: prepare_kernel(
            *refs, devices=devices, capacity=capacity, pitch=pitch, size_x=size_x, size_y=size_y
        ),
        (shape(devices * pitch, width),) + (shape(4, size_y, size_z),) * 2 + (shape(4, size_x, size_z),) * 2,
        scratch=[
            buffer(rows_dev, width), pltpu.VMEM((1, rows_dev), jnp.int32),
            pltpu.VMEM((1, rows_dev), jnp.int32), buffer(2, 4, size_y, size_z),
            buffer(2, 4, size_x, 8, size_z), buffer(devices * pitch, width),
            buffer(4, size_x, size_z), buffer(4, size_x, size_z), sems(19),
        ],
        specs=whole(1, SMEM) + whole(5, HBM),
        limit=60,
    )(wall_count, wall_rows, wall_dest.reshape(1, rows_dev), wall_line.reshape(1, rows_dev),
      adjoint_temp, conductivity)
    got = exchange(packed.reshape(devices, pitch, width)).reshape(devices * pitch, width)
    ylo = lax.ppermute(high, "gy", up_y)
    yhi = lax.ppermute(low, "gy", down_y)
    xlo = lax.ppermute(above, "gx", up_x)
    xhi = lax.ppermute(below, "gx", down_x)

    early = None
    if early_rows:
        early = call(
            lambda *refs: early_kernel(*refs, tile_rows=tile_rows, early_rows=early_rows, groups=1),
            shape(devices, 3, early_rows, size_z),
            scratch=[buffer(devices, 3, early_rows, size_z), sems(1), pltpu.SemaphoreType.DMA(())],
            specs=whole(1, SMEM) + whole(1, HBM),
        )(tile_owner, expand)
        early = exchange(early)

    rim_rows = (size_x + 2) * 8
    wide = buffer(size_x + 2, size_y, size_z)
    plane, flat_plane = buffer(size_x, size_y, size_z), buffer(cells, size_z)
    stack, rims = buffer(3, cells, size_z), (4, pieces, rim_rows, LANES)
    first_call = call(
        lambda *refs: first_kernel(
            *refs, devices=devices, size_x=size_x, size_y=size_y, capacity=capacity, pitch=pitch,
            step=cells // 8, groups=GROUPS,
        ),
        (grid, grid, grid, shape(*rims), lines, lines),
        scratch=[flat_plane, stack] + [flat_plane] * 4 + [buffer(*rims)] + [buffer(size_x, size_z)] * 2
        + [wide] * 5 + [plane] * 2 + [
            buffer(2, 4, size_y, size_z), buffer(4, size_x, size_z), buffer(4, size_x, size_z),
            buffer(devices * pitch, width), pltpu.VMEM((devices * pitch, 2 * width), BF16),
            buffer(pieces, cells, LANES), sems(6 + 4 * GROUPS),
        ],
        specs=whole(8, HBM),
        limit=60,
    )
    first, total, rate, krim, low, high = first_call(temp, cond, load, xlo, xhi, ylo, yhi, got)
    fylo = lax.ppermute(high, "gy", up_y)
    fyhi = lax.ppermute(low, "gy", down_y)
    sides = [buffer(size_x, size_z)] * 2
    edge = shape(size_y + 8, size_z)
    below, above = call(
        lambda *refs: planes_kernel(*refs, size_x=size_x, size_y=size_y),
        (edge, edge),
        scratch=sides + [buffer(2, size_y + 8, size_z), sems(4)],
        specs=whole(3, HBM),
    )(first, fylo, fyhi)
    fxlo = lax.ppermute(above, "gx", up_x)
    fxhi = lax.ppermute(below, "gx", down_x)

    late_rows = early_rows + 3 * kept
    field, late = call(
        lambda *refs: field_kernel(
            *refs, size_x=size_x, size_y=size_y, tile_rows=tile_rows, early_rows=early_rows,
            groups=GROUPS,
        ),
        (grid, shape(devices, late_rows, size_z)),
        scratch=[flat_plane, stack] + [flat_plane] * 3 + [stack, flat_plane]
        + [buffer(devices, late_rows, size_z), buffer(2, 4, size_y, size_z), buffer(*rims)] + sides
        + [buffer(2, size_y + 8, size_z)] + [wide] * 4 + [plane]
        + [sems(11 + 2 * GROUPS), pltpu.SemaphoreType.DMA(())],
        specs=whole(1, SMEM) + whole(13, HBM),
        limit=60,
    )(tile_owner, first, cond, rate, total, flat(ref_temp), expand, xlo, xhi, krim, fylo, fyhi, fxlo, fxhi)

    moved = exchange(late)
    tile_cells = tile_rows * size_z
    received = [(moved.reshape(devices * late_rows, size_z), late_rows)]
    if early_rows:
        received.append((early.reshape(devices * 3 * early_rows, size_z), 3 * early_rows))
    block_load = pl.pallas_call(
        lambda *refs: settle_kernel(*refs, tile_rows=tile_rows, early_rows=early_rows, pieces=pieces),
        out_shape=shape(1, 3, devices, tile_cells),
        grid=(devices // 8,),
        in_specs=[
            pl.BlockSpec((8 * rows, LANES), lambda b, p=p: (b, p)) for _, rows in received for p in range(pieces)
        ],
        out_specs=pl.BlockSpec((1, 3, 8, tile_cells), lambda b: (0, 0, b, 0)),
        compiler_params=pltpu.CompilerParams(vmem_limit_bytes=12 * MIB),
        name="settle",
    )(*[array for array, _ in received for _ in range(pieces)])
    return field.reshape(size_x, size_y, size_z), block_load


def solution(mesh):
    placed = (
        P("gx", "gy", None),
        P("gx", "gy", None),
        P(None, "gx", "gy", None),
        P(None, "gx", "gy", None),
        P("gx", "gy", None),
        P(("gx", "gy"), None),
        P(("gx", "gy"), None),
        P(("gx", "gy")),
        P(("gx", "gy")),
        P(("gx", "gy"), None),
    )

    return jax.shard_map(
        body,
        mesh=mesh,
        in_specs=placed,
        out_specs=(P("gx", "gy", None), P(("gx", "gy"), None, None, None)),
        check_vma=False,
    )
```
